32 devices in a mesh: dp: 8 (over z, x), mp: 4 (over y, core).
Axes of the slice: x: 2, y: 2, z: 4, core: 2. Of those that a mesh axis runs over, the one named last changes fastest.
Arguments:
- interface: float32 [8192, 512], P(('dp', 'mp')), may hold values from -6 to 6
- latents: float32 [1024, 1024], P(('dp', 'mp')), may hold values from -6 to 6
- keep_mask: int32 [8, 1024], P('dp'), may hold values from 0 to 1, as said below
- read_gain_lat: float32 [1024], replicated, may hold values from 0.25 to 1.75
- read_gain_int: float32 [512], replicated, may hold values from 0.25 to 1.75
- read_query: float32 [1024, 1024], P(None, 'mp'), may hold values from -0.1875 to 0.1875
- read_keyval: float32 [2, 512, 1024], P(None, None, 'mp'), may hold values from -0.25 to 0.25
- read_out: float32 [1024, 1024], P('mp'), may hold values from -3 to 3
- read_gain_mlp: float32 [1024], replicated, may hold values from 0.25 to 1.75
- read_up: float32 [1024, 4096], P(None, 'mp'), may hold values from -0.1875 to 0.1875
- read_down: float32 [4096, 1024], P('mp'), may hold values from -0.09375 to 0.09375
- self_gain_att: float32 [2, 1024], replicated, may hold values from 0.25 to 1.75
- self_qkv: float32 [2, 3, 1024, 1024], P(None, None, None, 'mp'), may hold values from -0.1875 to 0.1875
- self_out: float32 [2, 1024, 1024], P(None, 'mp'), may hold values from -1.5 to 1.5
- self_gain_mlp: float32 [2, 1024], replicated, may hold values from 0.25 to 1.75
- self_up: float32 [2, 1024, 4096], P(None, None, 'mp'), may hold values from -0.1875 to 0.1875
- self_down: float32 [2, 4096, 1024], P(None, 'mp'), may hold values from -0.09375 to 0.09375
- write_gain_int: float32 [512], replicated, may hold values from 0.25 to 1.75
- write_gain_lat: float32 [1024], replicated, may hold values from 0.25 to 1.75
- write_query: float32 [512, 512], P(None, 'mp'), may hold values from -0.25 to 0.25
- write_keyval: float32 [2, 1024, 512], P(None, None, 'mp'), may hold values from -0.1875 to 0.1875
- write_out: float32 [512, 512], P('mp'), may hold values from -1.5 to 1.5
- write_gain_mlp: float32 [512], replicated, may hold values from 0.25 to 1.75
- write_up: float32 [512, 2048], P(None, 'mp'), may hold values from -0.25 to 0.25
- write_down: float32 [2048, 512], P('mp'), may hold values from -0.125 to 0.125
- grad_interface_out: float32 [8192, 512], P(('dp', 'mp')), may hold values from -6 to 6
- grad_latents_out: float32 [1024, 1024], P(('dp', 'mp')), may hold values from -6 to 6
Outputs:
- interface_out: float32 [8192, 512], P(('dp', 'mp'))
- latents_out: float32 [1024, 1024], P(('dp', 'mp'))
- grad_interface: float32 [8192, 512], P(('dp', 'mp'))
- grad_latents: float32 [1024, 1024], P(('dp', 'mp'))
- grad_read_gain_lat: float32 [1024], replicated
- grad_read_gain_int: float32 [512], replicated
- grad_read_query: float32 [1024, 1024], P(None, 'mp')
- grad_read_keyval: float32 [2, 512, 1024], P(None, None, 'mp')
- grad_read_out: float32 [1024, 1024], P('mp')
- grad_read_gain_mlp: float32 [1024], replicated
- grad_read_up: float32 [1024, 4096], P(None, 'mp')
- grad_read_down: float32 [4096, 1024], P('mp')
- grad_self_gain_att: float32 [2, 1024], replicated
- grad_self_qkv: float32 [2, 3, 1024, 1024], P(None, None, None, 'mp')
- grad_self_out: float32 [2, 1024, 1024], P(None, 'mp')
- grad_self_gain_mlp: float32 [2, 1024], replicated
- grad_self_up: float32 [2, 1024, 4096], P(None, None, 'mp')
- grad_self_down: float32 [2, 4096, 1024], P(None, 'mp')
- grad_write_gain_int: float32 [512], replicated
- grad_write_gain_lat: float32 [1024], replicated
- grad_write_query: float32 [512, 512], P(None, 'mp')
- grad_write_keyval: float32 [2, 1024, 512], P(None, None, 'mp')
- grad_write_out: float32 [512, 512], P('mp')
- grad_write_gain_mlp: float32 [512], replicated
- grad_write_up: float32 [512, 2048], P(None, 'mp')
- grad_write_down: float32 [2048, 512], P('mp')
The draws below stay inside these ranges and needn't reach their ends.
Inputs may be any that keep to these rules, and one draw needn't show every extreme that they name: `keep_mask`: each image keeps one patch or more.
All inputs are finite; a program needn't handle non-finite values.
Results may differ from the reference program's by a relative error of at most 0.0003.
Values sent between devices are 32-bit elements; how exact they have to be, the bound alone decides.
No kernel may reach another device: no remote copies, remote signals or barrier semaphores. Data moves between devices by JAX's collectives and lax.ppermute only.
A program may use at most 256 MiB of HBM per device.

```python
import math
import jax
import jax.numpy as jnp
from jax import lax

D = 1024
E = 512
HEADS = 16
LATENTS = 128
PATCHES = 1024
LAYERS = 2
IMAGES = 8
FFL = 4096
FFI = 2048


def draw_keep_mask(key, part):
    level_key, bits_key, spot_key = jax.random.split(key, 3)
    levels = jax.random.randint(level_key, (IMAGES, 1), 150, 950)
    random_bits = jax.random.randint(bits_key, (IMAGES, PATCHES), 0, 1000)
    spots = jax.random.randint(spot_key, (IMAGES, 1), 0, PATCHES)
    places = jnp.arange(PATCHES)[None, :]
    return jnp.logical_or(random_bits < levels, places == spots).astype(jnp.int32)


def block_scale(own_key, dims, cuts, smallest, largest):
    gain = 1.0
    for axis_at, parts in cuts:
        steps = jax.random.uniform(jax.random.fold_in(jax.random.fold_in(own_key, 6), axis_at), (parts,), jnp.float32, smallest / len(cuts), largest / len(cuts))
        gain = gain * jnp.repeat(jnp.exp(steps), dims[axis_at] // parts).reshape((-1,) + (1,) * (len(dims) - 1 - axis_at))
    return gain


def bell_draw(own_key, dims, deviation, limit, cuts=(), kind=jnp.bfloat16):
    values = deviation * jax.random.normal(own_key, dims, jnp.float32)
    if cuts:
        values = values * block_scale(own_key, dims, cuts, -0.22, 0.18)
    return jnp.clip(values, -limit, limit).astype(kind)


def setup_inputs(seed: int = 0) -> dict:
    seeds = jax.random.split(jax.random.key(seed), 28)
    interface = bell_draw(seeds[0], (IMAGES * PATCHES, E), 1.0, 6.0, ((0, 32),), jnp.float32)
    latents = bell_draw(seeds[1], (IMAGES * LATENTS, D), 1.0, 6.0, ((0, 32),), jnp.float32)
    keep_mask = draw_keep_mask(jax.random.fold_in(seeds[27], 71), 0)
    read_gain_lat = jnp.clip(1.0 + 0.15 * jax.random.normal(seeds[3], (D,), jnp.float32), 0.25, 1.75)
    read_gain_int = jnp.clip(1.0 + 0.15 * jax.random.normal(seeds[4], (E,), jnp.float32), 0.25, 1.75)
    read_query = bell_draw(seeds[5], (D, D), D ** -0.5, 0.1875, ((1, 4),), jnp.float32)
    read_keyval = bell_draw(seeds[6], (2, E, D), E ** -0.5, 0.25, ((2, 4),), jnp.float32)
    read_out = bell_draw(seeds[7], (D, D), (max(1, D // 256)) ** -0.5, 3.0, ((0, 4),), jnp.float32)
    read_gain_mlp = jnp.clip(1.0 + 0.15 * jax.random.normal(seeds[8], (D,), jnp.float32), 0.25, 1.75)
    read_up = bell_draw(seeds[9], (D, FFL), D ** -0.5, 0.1875, ((1, 4),), jnp.float32)
    read_down = bell_draw(seeds[10], (FFL, D), FFL ** -0.5, 0.09375, ((0, 4),), jnp.float32)
    self_gain_att = jnp.clip(1.0 + 0.15 * jax.random.normal(seeds[11], (LAYERS, D), jnp.float32), 0.25, 1.75)
    self_qkv = bell_draw(seeds[12], (LAYERS, 3, D, D), D ** -0.5, 0.1875, ((3, 4),), jnp.float32)
    self_out = bell_draw(seeds[13], (LAYERS, D, D), (max(1, D // 64)) ** -0.5, 1.5, ((1, 4),), jnp.float32)
    self_gain_mlp = jnp.clip(1.0 + 0.15 * jax.random.normal(seeds[14], (LAYERS, D), jnp.float32), 0.25, 1.75)
    self_up = bell_draw(seeds[15], (LAYERS, D, FFL), D ** -0.5, 0.1875, ((2, 4),), jnp.float32)
    self_down = bell_draw(seeds[16], (LAYERS, FFL, D), FFL ** -0.5, 0.09375, ((1, 4),), jnp.float32)
    write_gain_int = jnp.clip(1.0 + 0.15 * jax.random.normal(seeds[17], (E,), jnp.float32), 0.25, 1.75)
    write_gain_lat = jnp.clip(1.0 + 0.15 * jax.random.normal(seeds[18], (D,), jnp.float32), 0.25, 1.75)
    write_query = bell_draw(seeds[19], (E, E), E ** -0.5, 0.25, ((1, 4),), jnp.float32)
    write_keyval = bell_draw(seeds[20], (2, D, E), D ** -0.5, 0.1875, ((2, 4),), jnp.float32)
    write_out = bell_draw(seeds[21], (E, E), (max(1, E // 32)) ** -0.5, 1.5, ((0, 4),), jnp.float32)
    write_gain_mlp = jnp.clip(1.0 + 0.15 * jax.random.normal(seeds[22], (E,), jnp.float32), 0.25, 1.75)
    write_up = bell_draw(seeds[23], (E, FFI), E ** -0.5, 0.25, ((1, 4),), jnp.float32)
    write_down = bell_draw(seeds[24], (FFI, E), FFI ** -0.5, 0.125, ((0, 4),), jnp.float32)
    grad_interface_out = bell_draw(seeds[25], (IMAGES * PATCHES, E), 1.0, 6.0, ((0, 32),), jnp.float32)
    grad_latents_out = bell_draw(seeds[26], (IMAGES * LATENTS, D), 1.0, 6.0, ((0, 32),), jnp.float32)
    return {"interface": interface, "latents": latents, "keep_mask": keep_mask, "read_gain_lat": read_gain_lat, "read_gain_int": read_gain_int, "read_query": read_query, "read_keyval": read_keyval, "read_out": read_out, "read_gain_mlp": read_gain_mlp, "read_up": read_up, "read_down": read_down, "self_gain_att": self_gain_att, "self_qkv": self_qkv, "self_out": self_out, "self_gain_mlp": self_gain_mlp, "self_up": self_up, "self_down": self_down, "write_gain_int": write_gain_int, "write_gain_lat": write_gain_lat, "write_query": write_query, "write_keyval": write_keyval, "write_out": write_out, "write_gain_mlp": write_gain_mlp, "write_up": write_up, "write_down": write_down, "grad_interface_out": grad_interface_out, "grad_latents_out": grad_latents_out}


@jax.custom_vjp
def low(v):
    return lax.optimization_barrier(v.astype(jnp.bfloat16)).astype(jnp.float32)

@jax.custom_vjp
def low_back(v):
    return v

def low_keep(v):
    return (low(v), None)

def low_pass(kept, grad):
    return (grad,)

def back_keep(v):
    return (v, None)

def back_low(kept, grad):
    return (low(grad),)
low.defvjp(low_keep, low_pass)
low_back.defvjp(back_keep, back_low)
EPSILON = 1e-05
PRECISE = lax.Precision.HIGHEST
MASK_FILL = -1000000000.0

def layer_norm(values, gain_vec):
    centre = lax.optimization_barrier(jnp.mean(values, axis=-1, keepdims=True))
    centred = values - centre
    spread = lax.optimization_barrier(jnp.mean(centred * centred, axis=-1, keepdims=True))
    return centred * lax.rsqrt(spread + EPSILON) * gain_vec

def product(left_side, right_side):
    return jnp.dot(left_side, right_side, precision=PRECISE)

def attention(queries, keys_in, values_in, key_bias, images, head_width):
    query_len = queries.shape[0] // images
    key_len = keys_in.shape[0] // images
    head_count = queries.shape[1] // head_width
    query_heads = queries.reshape(images, query_len, head_count, head_width)
    key_heads = keys_in.reshape(images, key_len, head_count, head_width)
    value_heads = values_in.reshape(images, key_len, head_count, head_width)
    scores = jnp.einsum('bqhd,bkhd->bhqk', query_heads, key_heads, precision=PRECISE)
    scores = scores / math.sqrt(head_width) + key_bias[:, None, None, :]
    weights = jax.nn.softmax(scores, axis=-1)
    mixture = jnp.einsum('bhqk,bkhd->bqhd', weights, value_heads, precision=PRECISE)
    return mixture.reshape(images * query_len, head_count * head_width)

def image_attention(queries, keys_in, values_in, key_bias, head_width):
    images = key_bias.shape[0]
    query_len = queries.shape[0] // images
    key_len = keys_in.shape[0] // images
    width_all = queries.shape[1]

    def single(pieces):
        return attention(pieces[0], pieces[1], pieces[2], pieces[3][None, :], 1, head_width)
    stacked = (queries.reshape(images, query_len, width_all), keys_in.reshape(images, key_len, width_all), values_in.reshape(images, key_len, width_all), key_bias)
    result = lax.map(jax.checkpoint(single), stacked)
    return result.reshape(images * query_len, width_all)

def branch_attend(query_src, key_src, query_gain, key_gain, w_query, w_key, w_value, w_out, key_bias, head_width):
    query_norm = layer_norm(query_src, query_gain)
    key_norm = layer_norm(key_src, key_gain)
    mixture = image_attention(product(query_norm, w_query), product(key_norm, w_key), product(key_norm, w_value), key_bias, head_width)
    return query_src + product(mixture, w_out)

def branch_expand(stream, gain_vec, w_up, w_down):
    hidden = jax.nn.gelu(product(layer_norm(stream, gain_vec), w_up))
    return stream + product(hidden, w_down)

def forward(keep_mask, interface, latents, read_gain_lat, read_gain_int, read_query, read_keyval, read_out, read_gain_mlp, read_up, read_down, self_gain_att, self_qkv, self_out, self_gain_mlp, self_up, self_down, write_gain_int, write_gain_lat, write_query, write_keyval, write_out, write_gain_mlp, write_up, write_down):
    images = keep_mask.shape[0]
    keep_rows = keep_mask.reshape(-1, 1).astype(interface.dtype)
    stream_x = interface * keep_rows
    read_bias = jnp.where(keep_mask > 0, 0.0, MASK_FILL).astype(interface.dtype)
    open_bias = jnp.zeros((images, LATENTS), interface.dtype)
    stream_z = branch_attend(latents, stream_x, read_gain_lat, read_gain_int, read_query, read_keyval[0], read_keyval[1], read_out, read_bias, D // HEADS)
    stream_z = branch_expand(stream_z, read_gain_mlp, read_up, read_down)
    for layer_idx in range(LAYERS):
        stream_z = branch_attend(stream_z, stream_z, self_gain_att[layer_idx], self_gain_att[layer_idx], self_qkv[layer_idx, 0], self_qkv[layer_idx, 1], self_qkv[layer_idx, 2], self_out[layer_idx], open_bias, D // HEADS)
        stream_z = branch_expand(stream_z, self_gain_mlp[layer_idx], self_up[layer_idx], self_down[layer_idx])
    stream_x = branch_attend(stream_x, stream_z, write_gain_int, write_gain_lat, write_query, write_keyval[0], write_keyval[1], write_out, open_bias, E // HEADS)
    stream_x = branch_expand(stream_x, write_gain_mlp, write_up, write_down)
    return (stream_x, stream_z)

def reference(interface, latents, keep_mask, read_gain_lat, read_gain_int, read_query, read_keyval, read_out, read_gain_mlp, read_up, read_down, self_gain_att, self_qkv, self_out, self_gain_mlp, self_up, self_down, write_gain_int, write_gain_lat, write_query, write_keyval, write_out, write_gain_mlp, write_up, write_down, grad_interface_out, grad_latents_out):

    def run_block(interface_in, latents_in, p02, p03, p04, p05, p06, p07, p08, p09, p10, p11, p12, p13, p14, p15, p16, p17, p18, p19, p20, p21, p22, p23):
        return forward(keep_mask, interface_in, latents_in, p02, p03, p04, p05, p06, p07, p08, p09, p10, p11, p12, p13, p14, p15, p16, p17, p18, p19, p20, p21, p22, p23)
    outputs, pull_back = jax.vjp(run_block, interface, latents, read_gain_lat, read_gain_int, read_query, read_keyval, read_out, read_gain_mlp, read_up, read_down, self_gain_att, self_qkv, self_out, self_gain_mlp, self_up, self_down, write_gain_int, write_gain_lat, write_query, write_keyval, write_out, write_gain_mlp, write_up, write_down)
    gradients = pull_back((grad_interface_out, grad_latents_out))
    return (outputs[0], outputs[1], gradients[0], gradients[1], gradients[2], gradients[3], gradients[4], gradients[5], gradients[6], gradients[7], gradients[8], gradients[9], gradients[10], gradients[11], gradients[12], gradients[13], gradients[14], gradients[15], gradients[16], gradients[17], gradients[18], gradients[19], gradients[20], gradients[21], gradients[22], gradients[23])
```

```python
import functools
import math

import jax
import jax.numpy as jnp
from jax import lax
from jax.experimental import pallas as pl
from jax.experimental.pallas import tpu as pltpu
from jax.sharding import PartitionSpec as P

EPSILON = 1e-05
BF16 = jnp.bfloat16
F32 = jnp.float32
NN = (((1,), (0,)), ((), ()))
NT = (((1,), (1,)), ((), ()))
TN = (((0,), (0,)), ((), ()))
GELU_C = math.sqrt(2.0 / math.pi)
HEAD = 64
VMEM_BYTES = 58 * 1024 * 1024


def cut(value):
    high = value.astype(BF16)
    return high, (value - high.astype(F32)).astype(BF16)


def mul3(left, right, dims):
    one = functools.partial(lax.dot_general, dimension_numbers=dims, preferred_element_type=F32)
    return one(left[0], right[0]) + (one(left[1], right[0]) + one(left[0], right[1]))


def normed(value):
    centre = jnp.mean(value, axis=-1, keepdims=True)
    centred = value - centre
    scale = lax.rsqrt(jnp.mean(centred * centred, axis=-1, keepdims=True) + EPSILON)
    return centred * scale, scale


def norm_back(dy, value, gain):
    n, scale = normed(value)
    dn = dy * gain
    dv = (
        dn
        - jnp.mean(dn, axis=-1, keepdims=True)
        - n * jnp.mean(dn * n, axis=-1, keepdims=True)
    ) * scale
    return dv, jnp.sum(dy * n, axis=0, keepdims=True)


def gelu_parts(pre):
    square = pre * pre
    bend = jnp.tanh(GELU_C * pre * (1.0 + 0.044715 * square))
    half = 0.5 * (1.0 + bend)
    slope = half + 0.5 * pre * (1.0 - bend * bend) * (GELU_C * (1.0 + 3.0 * 0.044715 * square))
    return pre * half, slope


def head_masks(width, head):
    lane = lax.broadcasted_iota(jnp.int32, (1, width), 1)
    return [(lane // head == h).astype(F32) for h in range(width // head)]


def stack_heads(value, masks):
    return jnp.concatenate([value * mask for mask in masks], axis=0)


def merge_heads(stacked, masks):
    rows = stacked.shape[0] // len(masks)
    total = stacked[:rows] * masks[0]
    for h in range(1, len(masks)):
        total = total + stacked[h * rows : (h + 1) * rows] * masks[h]
    return total


def soft(scores):
    top = jnp.max(scores, axis=-1, keepdims=True)
    raised = jnp.exp(scores - top)
    return raised / jnp.sum(raised, axis=-1, keepdims=True)


def attend(q, k, v, masks, head, bias=None):
    qs = stack_heads(q, masks)
    scores = mul3(cut(qs), cut(k), NT) * (1.0 / math.sqrt(head))
    if bias is not None:
        scores = scores + bias
    p = soft(scores)
    return merge_heads(mul3(cut(p), cut(v), NN), masks), p, qs


def attend_back(q, k, v, do, masks, head):
    scale = 1.0 / math.sqrt(head)
    k2, v2 = cut(k), cut(v)
    qs = cut(stack_heads(q, masks))
    p = soft(mul3(qs, k2, NT) * scale)
    p2 = cut(p)
    mix = merge_heads(mul3(p2, v2, NN), masks)
    dos = cut(stack_heads(do, masks))
    dp = mul3(dos, v2, NT)
    ds = cut(p * (dp - jnp.sum(dp * p, axis=-1, keepdims=True)) * scale)
    dq = merge_heads(mul3(ds, k2, NN), masks)
    dk = mul3(ds, qs, TN)
    dv = mul3(p2, dos, TN)
    return mix, dq, dk, dv


def place_copies(where, sets, hi, lo, half, stage, sem):
    z_at, x_at, c_at = where[0], where[1], where[2]
    copies = []
    for flip_c in range(2):
        for flip_x in range(lo):
            ref = sets[flip_c * lo + flip_x]
            for d in range(hi):
                image = lax.rem(z_at + d, hi) * lo + lax.rem(x_at + flip_x, lo)
                row = (image * 2 + lax.rem(c_at + flip_c, 2)) * half
                row = pl.multiple_of(row, half)
                copies.append(
                    pltpu.make_async_copy(ref.at[d], stage.at[pl.ds(row, half)], sem)
                )
    return copies


def load_rows(where, z_sets, d_sets, gain, hi, lo, half, stage_z, stage_d, a, at, d2, sems):
    zc = place_copies(where, z_sets, hi, lo, half, stage_z, sems.at[0])
    dc = place_copies(where, d_sets, hi, lo, half, stage_d, sems.at[1])
    for one in zc:
        one.start()
    for one in dc:
        one.start()
    for one in zc:
        one.wait()
    rows = stage_z.shape[0]
    step = 128

    def norm_step(i, carry):
        at_rows = pl.ds(pl.multiple_of(i * step, step), step)
        n = normed(stage_z[at_rows, :])[0] * gain[...]
        a[0, at_rows, :], a[1, at_rows, :] = cut(n)
        at[0, :, at_rows], at[1, :, at_rows] = cut(n.T)
        return carry

    lax.fori_loop(0, rows // step, norm_step, 0)
    for one in dc:
        one.wait()

    def cut_step(i, carry):
        at_rows = pl.ds(pl.multiple_of(i * step, step), step)
        d2[0, at_rows, :], d2[1, at_rows, :] = cut(stage_d[at_rows, :])
        return carry

    lax.fori_loop(0, rows // step, cut_step, 0)


def mlp_weights_kernel(hi, lo, half, *refs):
    where = refs[0]
    z_sets, d_sets = refs[1:5], refs[5:9]
    gain, w_up, w_down = refs[9:12]
    g_up, g_down, stage_z, stage_d, a, at, d2, h2t, du2, sems = refs[-10:]
    rows = stage_z.shape[0]
    tile = w_up.shape[1]
    step = 256

    @pl.when(pl.program_id(0) == 0)
    def _():
        load_rows(where, z_sets, d_sets, gain, hi, lo, half, stage_z, stage_d, a, at, d2, sems)

    wu = cut(w_up[...])
    wd = cut(w_down[...])

    def rows_step(i, carry):
        r = pl.ds(pl.multiple_of(i * step, step), step)
        pre = mul3((a[0, r, :], a[1, r, :]), wu, NN)
        hidden, slope = gelu_parts(pre)
        du = mul3((d2[0, r, :], d2[1, r, :]), wd, NT) * slope
        du2[0, r, :], du2[1, r, :] = cut(du)
        h2t[0, :, r], h2t[1, :, r] = cut(hidden.T)
        return carry

    lax.fori_loop(0, rows // step, rows_step, 0)
    du = (du2[0], du2[1])
    width = g_up.shape[0]

    def up_step(i, carry):
        r = pl.ds(pl.multiple_of(i * step, step), step)
        g_up[r, :] = mul3((at[0, r, :], at[1, r, :]), du, NN)
        return carry

    lax.fori_loop(0, width // step, up_step, 0)
    ht = (h2t[0], h2t[1])

    def down_step(i, carry):
        r = pl.ds(pl.multiple_of(i * step, step), step)
        g_down[:, r] = mul3(ht, (d2[0, :, r], d2[1, :, r]), NN)
        return carry

    lax.fori_loop(0, width // step, down_step, 0)


def mlp_weights(where, z_sets, d_sets, gain, w_up, w_down, layer, before):
    hi, half, width = z_sets[0].shape
    lo = 2
    rows = hi * lo * 2 * half
    layers, _, hid = w_up.shape
    tile = 256
    flops = 3 * 2 * 4 * rows * width * hid
    call = pl.pallas_call(
        functools.partial(mlp_weights_kernel, hi, lo, half),
        grid=(hid // tile,),
        in_specs=[pl.BlockSpec(memory_space=pltpu.SMEM)]
        + [pl.BlockSpec(memory_space=pl.ANY)] * 8
        + [
            pl.BlockSpec((1, width), lambda j: (0, 0)),
            pl.BlockSpec((None, width, tile), lambda j: (layer, 0, j)),
            pl.BlockSpec((None, tile, width), lambda j: (layer, j, 0)),
        ]
        + [pl.BlockSpec(memory_space=pl.ANY)] * len(before),
        out_specs=[
            pl.BlockSpec((None, width, tile), lambda j: (layer, 0, j)),
            pl.BlockSpec((None, tile, width), lambda j: (layer, j, 0)),
        ],
        out_shape=[
            jax.ShapeDtypeStruct((layers, width, hid), F32),
            jax.ShapeDtypeStruct((layers, hid, width), F32),
        ],
        input_output_aliases={12 + i: i for i in range(len(before))},
        scratch_shapes=[
            pltpu.VMEM((rows, width), F32),
            pltpu.VMEM((rows, width), F32),
            pltpu.VMEM((2, rows, width), BF16),
            pltpu.VMEM((2, width, rows), BF16),
            pltpu.VMEM((2, rows, width), BF16),
            pltpu.VMEM((2, tile, rows), BF16),
            pltpu.VMEM((2, rows, tile), BF16),
            pltpu.SemaphoreType.DMA((2,)),
        ],
        compiler_params=pltpu.CompilerParams(vmem_limit_bytes=VMEM_BYTES),
        cost_estimate=pl.CostEstimate(
            flops=flops, bytes_accessed=4 * (2 * rows * width + 4 * width * hid), transcendentals=rows * hid
        ),
        name="mlp_weights",
    )
    return call(where, *z_sets, *d_sets, gain.reshape(1, width), w_up, w_down, *before)


def att_weights_kernel(hi, lo, half, *refs):
    where = refs[0]
    z_sets, d_sets = refs[1:5], refs[5:9]
    gain, w_qkv, w_out = refs[9:12]
    g_qkv, g_out, stage_z, stage_d, a, at, d2, qkv, do, mixt, sems = refs[-11:]
    rows = stage_z.shape[0]
    image_rows = 2 * half
    cols = w_out.shape[0]
    step = 256
    load_rows(where, z_sets, d_sets, gain, hi, lo, half, stage_z, stage_d, a, at, d2, sems)
    for part in range(3):
        w = cut(w_qkv[part])

        def in_step(i, carry, part=part, w=w):
            r = pl.ds(pl.multiple_of(i * step, step), step)
            qkv[part, r, :] = mul3((a[0, r, :], a[1, r, :]), w, NN)
            return carry

        lax.fori_loop(0, rows // step, in_step, 0)
    wo = cut(w_out[...])

    def do_step(i, carry):
        r = pl.ds(pl.multiple_of(i * step, step), step)
        do[r, :] = mul3((d2[0, r, :], d2[1, r, :]), wo, NT)
        return carry

    lax.fori_loop(0, rows // step, do_step, 0)
    masks = head_masks(cols, HEAD)

    def image_step(i, carry):
        r = pl.ds(pl.multiple_of(i * image_rows, image_rows), image_rows)
        mix, dq, dk, dv = attend_back(qkv[0, r, :], qkv[1, r, :], qkv[2, r, :], do[r, :], masks, HEAD)
        qkv[0, r, :] = dq
        qkv[1, r, :] = dk
        qkv[2, r, :] = dv
        mixt[0, :, r], mixt[1, :, r] = cut(mix.T)
        return carry

    lax.fori_loop(0, hi * lo, image_step, 0)
    width = stage_z.shape[1]
    for part in range(3):
        g = cut(qkv[part])

        def up_step(i, carry, part=part, g=g):
            r = pl.ds(pl.multiple_of(i * step, step), step)
            g_qkv[part, r, :] = mul3((at[0, r, :], at[1, r, :]), g, NN)
            return carry

        lax.fori_loop(0, width // step, up_step, 0)
    mt = (mixt[0], mixt[1])

    def out_step(i, carry):
        r = pl.ds(pl.multiple_of(i * step, step), step)
        g_out[:, r] = mul3(mt, (d2[0, :, r], d2[1, :, r]), NN)
        return carry

    lax.fori_loop(0, width // step, out_step, 0)


def att_weights(where, z_sets, d_sets, gain, w_qkv, w_out, layer, before):
    hi, half, width = z_sets[0].shape
    lo = 2
    rows = hi * lo * 2 * half
    layers, cols, _ = w_out.shape
    flops = 3 * 2 * 8 * rows * width * cols
    call = pl.pallas_call(
        functools.partial(att_weights_kernel, hi, lo, half),
        grid=(1,),
        in_specs=[pl.BlockSpec(memory_space=pltpu.SMEM)]
        + [pl.BlockSpec(memory_space=pl.ANY)] * 8
        + [
            pl.BlockSpec((1, width), lambda j: (0, 0)),
            pl.BlockSpec((None, 3, width, cols), lambda j: (layer, 0, 0, 0)),
            pl.BlockSpec((None, cols, width), lambda j: (layer, 0, 0)),
        ]
        + [pl.BlockSpec(memory_space=pl.ANY)] * len(before),
        out_specs=[
            pl.BlockSpec((None, 3, width, cols), lambda j: (layer, 0, 0, 0)),
            pl.BlockSpec((None, cols, width), lambda j: (layer, 0, 0)),
        ],
        out_shape=[
            jax.ShapeDtypeStruct((layers, 3, width, cols), F32),
            jax.ShapeDtypeStruct((layers, cols, width), F32),
        ],
        input_output_aliases={12 + i: i for i in range(len(before))},
        scratch_shapes=[
            pltpu.VMEM((rows, width), F32),
            pltpu.VMEM((rows, width), F32),
            pltpu.VMEM((2, rows, width), BF16),
            pltpu.VMEM((2, width, rows), BF16),
            pltpu.VMEM((2, rows, width), BF16),
            pltpu.VMEM((3, rows, cols), F32),
            pltpu.VMEM((rows, cols), F32),
            pltpu.VMEM((2, cols, rows), BF16),
            pltpu.SemaphoreType.DMA((2,)),
        ],
        compiler_params=pltpu.CompilerParams(vmem_limit_bytes=VMEM_BYTES),
        cost_estimate=pl.CostEstimate(
            flops=flops, bytes_accessed=4 * (2 * rows * width + 8 * width * cols), transcendentals=rows * 512
        ),
        name="att_weights",
    )
    return call(where, *z_sets, *d_sets, gain.reshape(1, width), w_qkv, w_out, *before)


def put_halves(core, mine, other, full):
    half = mine.shape[0]
    full[pl.ds(pl.multiple_of(core * half, half), half), :] = mine[...]
    full[pl.ds(pl.multiple_of((1 - core) * half, half), half), :] = other[...]


def get_halves(core, full, mine, other):
    half = mine.shape[0]
    mine[...] = full[pl.ds(pl.multiple_of(core * half, half), half), :]
    if other is not None:
        other[...] = full[pl.ds(pl.multiple_of((1 - core) * half, half), half), :]


def mul3_few(left, right, dims):
    rows = left[0].shape[0]
    one = functools.partial(lax.dot_general, dimension_numbers=dims, preferred_element_type=F32)
    both = one(jnp.concatenate([left[0], left[1]], axis=0), right[0])
    return (both[:rows] + both[rows:]) + one(left[0], right[1])


def mlp_forward_kernel(where, z_ref, w_ref, wo_ref, gain, w_up, w_down,
                       z_out, z_half, pre_out, mine, other, a, acc):
    core = where[2]
    j = pl.program_id(0)

    @pl.when(j == 0)
    def _():
        put_halves(core, w_ref, wo_ref, acc)
        z_new = z_ref[...] + acc[...]
        z_out[...] = z_new
        a[0], a[1] = cut(normed(z_new)[0] * gain[...])
        get_halves(core, z_out, z_half, None)
        acc[...] = jnp.zeros_like(acc)

    pre = mul3_few((a[0], a[1]), cut(w_up[...]), NN)
    pre_out[...] = pre
    hidden, _ = gelu_parts(pre)
    acc[...] += mul3_few(cut(hidden), cut(w_down[...]), NN)

    @pl.when(j == pl.num_programs(0) - 1)
    def _():
        get_halves(core, acc, mine, other)


def mlp_forward(where, z, w, wo, gain, w_up, w_down, layer):
    rows, width = z.shape
    half = rows // 2
    hid = w_up.shape[2]
    tile = 256
    whole = lambda shape: pl.BlockSpec(shape, lambda j: (0, 0))
    return pl.pallas_call(
        mlp_forward_kernel,
        grid=(hid // tile,),
        in_specs=[
            pl.BlockSpec(memory_space=pltpu.SMEM),
            whole((rows, width)),
            whole((half, width)),
            whole((half, width)),
            whole((1, width)),
            pl.BlockSpec((None, width, tile), lambda j: (layer, 0, j)),
            pl.BlockSpec((None, tile, width), lambda j: (layer, j, 0)),
        ],
        out_specs=[
            whole((rows, width)),
            whole((half, width)),
            pl.BlockSpec((rows, tile), lambda j: (0, j)),
            whole((half, width)),
            whole((half, width)),
        ],
        out_shape=[
            jax.ShapeDtypeStruct((rows, width), F32),
            jax.ShapeDtypeStruct((half, width), F32),
            jax.ShapeDtypeStruct((rows, hid), F32),
            jax.ShapeDtypeStruct((half, width), F32),
            jax.ShapeDtypeStruct((half, width), F32),
        ],
        scratch_shapes=[pltpu.VMEM((2, rows, width), BF16), pltpu.VMEM((rows, width), F32)],
        compiler_params=pltpu.CompilerParams(vmem_limit_bytes=VMEM_BYTES // 2),
        cost_estimate=pl.CostEstimate(
            flops=3 * 4 * rows * width * hid, bytes_accessed=8 * width * hid, transcendentals=rows * hid
        ),
        name="mlp_forward",
    )(where, z, w, wo, gain.reshape(1, width), w_up, w_down)


def att_forward_kernel(where, z_ref, w_ref, wo_ref, gain, w_qkv, w_out,
                       z_out, z_half, qkv_out, mine, other, acc):
    core = where[2]
    put_halves(core, w_ref, wo_ref, acc)
    z_new = z_ref[...] + acc[...]
    z_out[...] = z_new
    get_halves(core, z_out, z_half, None)
    a = cut(normed(z_new)[0] * gain[...])
    parts = []
    for part in range(3):
        one = mul3_few(a, cut(w_qkv[part]), NN)
        qkv_out[part] = one
        parts.append(one)
    masks = head_masks(w_out.shape[0], HEAD)
    mix, _, _ = attend(*parts, masks, HEAD)
    acc[...] = mul3_few(cut(mix), cut(w_out[...]), NN)
    get_halves(core, acc, mine, other)


def att_forward(where, z, w, wo, gain, w_qkv, w_out):
    rows, width = z.shape
    half = rows // 2
    cols = w_out.shape[0]
    vm = pl.BlockSpec(memory_space=pltpu.VMEM)
    return pl.pallas_call(
        att_forward_kernel,
        in_specs=[pl.BlockSpec(memory_space=pltpu.SMEM)] + [vm] * 6,
        out_specs=[vm] * 5,
        out_shape=[
            jax.ShapeDtypeStruct((rows, width), F32),
            jax.ShapeDtypeStruct((half, width), F32),
            jax.ShapeDtypeStruct((3, rows, cols), F32),
            jax.ShapeDtypeStruct((half, width), F32),
            jax.ShapeDtypeStruct((half, width), F32),
        ],
        scratch_shapes=[pltpu.VMEM((rows, width), F32)],
        compiler_params=pltpu.CompilerParams(vmem_limit_bytes=VMEM_BYTES // 2),
        cost_estimate=pl.CostEstimate(
            flops=3 * 8 * rows * width * cols, bytes_accessed=16 * width * cols, transcendentals=rows * 512
        ),
        name="att_forward",
    )(where, z, w, wo, gain.reshape(1, width), w_qkv, w_out)


def add_norm_back(core, d_ref, w_ref, wo_ref, z_ref, gain, d_out, d_half, g_out, acc):
    put_halves(core, w_ref, wo_ref, acc)
    dv, dg = norm_back(acc[...], z_ref[...], gain[...])
    g_out[...] = dg
    d_out[...] = d_ref[...] + dv
    get_halves(core, d_out, d_half, None)


def mlp_backward_kernel(where, d_ref, w_ref, wo_ref, z_ref, gain, pre, w_up, w_down,
                        d_out, d_half, g_out, mine, other, d2, acc):
    core = where[2]
    j = pl.program_id(0)

    @pl.when(j == 0)
    def _():
        add_norm_back(core, d_ref, w_ref, wo_ref, z_ref, gain, d_out, d_half, g_out, acc)
        d2[0], d2[1] = cut(d_out[...])
        acc[...] = jnp.zeros_like(acc)

    _, slope = gelu_parts(pre[...])
    du = mul3_few((d2[0], d2[1]), cut(w_down[...]), NT) * slope
    acc[...] += mul3_few(cut(du), cut(w_up[...]), NT)

    @pl.when(j == pl.num_programs(0) - 1)
    def _():
        get_halves(core, acc, mine, other)


def mlp_backward(where, d, w, wo, z_prev, gain_prev, pre, w_up, w_down, layer):
    rows, width = d.shape
    half = rows // 2
    hid = w_up.shape[2]
    tile = 256
    whole = lambda shape: pl.BlockSpec(shape, lambda j: (0, 0))
    return pl.pallas_call(
        mlp_backward_kernel,
        grid=(hid // tile,),
        in_specs=[
            pl.BlockSpec(memory_space=pltpu.SMEM),
            whole((rows, width)),
            whole((half, width)),
            whole((half, width)),
            whole((rows, width)),
            whole((1, width)),
            pl.BlockSpec((rows, tile), lambda j: (0, j)),
            pl.BlockSpec((None, width, tile), lambda j: (layer, 0, j)),
            pl.BlockSpec((None, tile, width), lambda j: (layer, j, 0)),
        ],
        out_specs=[
            whole((rows, width)),
            whole((half, width)),
            whole((1, width)),
            whole((half, width)),
            whole((half, width)),
        ],
        out_shape=[
            jax.ShapeDtypeStruct((rows, width), F32),
            jax.ShapeDtypeStruct((half, width), F32),
            jax.ShapeDtypeStruct((1, width), F32),
            jax.ShapeDtypeStruct((half, width), F32),
            jax.ShapeDtypeStruct((half, width), F32),
        ],
        scratch_shapes=[pltpu.VMEM((2, rows, width), BF16), pltpu.VMEM((rows, width), F32)],
        compiler_params=pltpu.CompilerParams(vmem_limit_bytes=VMEM_BYTES // 2),
        cost_estimate=pl.CostEstimate(
            flops=3 * 4 * rows * width * hid, bytes_accessed=8 * width * hid, transcendentals=rows * hid
        ),
        name="mlp_backward",
    )(where, d, w, wo, z_prev, gain_prev.reshape(1, width), pre, w_up, w_down)


def att_backward_kernel(where, d_ref, w_ref, wo_ref, z_ref, gain, qkv, w_qkv, w_out,
                        d_out, d_half, g_out, mine, other, acc):
    core = where[2]
    add_norm_back(core, d_ref, w_ref, wo_ref, z_ref, gain, d_out, d_half, g_out, acc)
    do = mul3_few(cut(d_out[...]), cut(w_out[...]), NT)
    masks = head_masks(w_out.shape[0], HEAD)
    _, dq, dk, dv = attend_back(qkv[0], qkv[1], qkv[2], do, masks, HEAD)
    acc[...] = mul3_few(cut(dq), cut(w_qkv[0]), NT)
    acc[...] += mul3_few(cut(dk), cut(w_qkv[1]), NT)
    acc[...] += mul3_few(cut(dv), cut(w_qkv[2]), NT)
    get_halves(core, acc, mine, other)


def att_backward(where, d, w, wo, z_prev, gain_prev, qkv, w_qkv, w_out):
    rows, width = d.shape
    half = rows // 2
    cols = w_out.shape[0]
    vm = pl.BlockSpec(memory_space=pltpu.VMEM)
    return pl.pallas_call(
        att_backward_kernel,
        in_specs=[pl.BlockSpec(memory_space=pltpu.SMEM)] + [vm] * 8,
        out_specs=[vm] * 5,
        out_shape=[
            jax.ShapeDtypeStruct((rows, width), F32),
            jax.ShapeDtypeStruct((half, width), F32),
            jax.ShapeDtypeStruct((1, width), F32),
            jax.ShapeDtypeStruct((half, width), F32),
            jax.ShapeDtypeStruct((half, width), F32),
        ],
        scratch_shapes=[pltpu.VMEM((rows, width), F32)],
        compiler_params=pltpu.CompilerParams(vmem_limit_bytes=VMEM_BYTES // 2),
        cost_estimate=pl.CostEstimate(
            flops=3 * 8 * rows * width * cols, bytes_accessed=16 * width * cols, transcendentals=rows * 512
        ),
        name="att_backward",
    )(where, d, w, wo, z_prev, gain_prev.reshape(1, width), qkv, w_qkv, w_out)


MASK_FILL = -1000000000.0
PRECISE = lax.Precision.HIGH
HEADS = 16


def layer_norm(values, gain_vec):
    centre = jnp.mean(values, axis=-1, keepdims=True)
    centred = values - centre
    spread = jnp.mean(centred * centred, axis=-1, keepdims=True)
    return centred * lax.rsqrt(spread + EPSILON) * gain_vec


def product(left_side, right_side):
    return jnp.dot(left_side, right_side, precision=PRECISE)


def contract_rows(left_side, right_side):
    return lax.dot_general(left_side, right_side, (((0,), (0,)), ((), ())), precision=PRECISE)


def contract_last(left_side, right_side):
    return lax.dot_general(left_side, right_side, (((1,), (1,)), ((), ())), precision=PRECISE)


def attention(queries, keys_in, values_in, key_bias, images, head_width):
    query_len = queries.shape[0] // images
    key_len = keys_in.shape[0] // images
    head_count = queries.shape[1] // head_width
    query_heads = queries.reshape(images, query_len, head_count, head_width)
    key_heads = keys_in.reshape(images, key_len, head_count, head_width)
    value_heads = values_in.reshape(images, key_len, head_count, head_width)
    scores = jnp.einsum("bqhd,bkhd->bhqk", query_heads, key_heads, precision=PRECISE)
    scores = scores / math.sqrt(head_width)
    if key_bias is not None:
        scores = scores + key_bias[:, None, None, :]
    weights = jax.nn.softmax(scores, axis=-1)
    mixture = jnp.einsum("bhqk,bkhd->bqhd", weights, value_heads, precision=PRECISE)
    return mixture.reshape(images * query_len, head_count * head_width)


def gelu_pair(pre):
    return jax.vjp(jax.nn.gelu, pre)


def make_body(dp, mp):
    ny = mp // 2
    lo = 2
    hi = dp // lo

    def mp_perm(fn):
        return [(i, fn(i)) for i in range(mp)]

    def core_swap(piece):
        return lax.ppermute(piece, "mp", mp_perm(lambda i: i ^ 1))

    def y_shift(piece, step):
        return lax.ppermute(piece, "mp", mp_perm(lambda i: (i + 2 * step) % mp))

    def core_idx():
        return lax.axis_index("mp") % 2

    def by_core(first, second, axis):
        core = core_idx()
        return jnp.where(
            core == 0,
            jnp.concatenate([first, second], axis),
            jnp.concatenate([second, first], axis),
        )

    def halves(partial):
        half = partial.shape[0] // 2
        core = core_idx()
        return (
            lax.dynamic_slice_in_dim(partial, core * half, half, 0),
            lax.dynamic_slice_in_dim(partial, (1 - core) * half, half, 0),
        )

    def sum_halves(mine, other):
        total = mine + core_swap(other)
        whole = total
        for step in range(1, ny):
            whole = whole + y_shift(total, step)
        return whole, core_swap(whole)

    def sum_rows(partial):
        rows = partial.shape[0] // mp
        core = core_idx()
        y_idx = lax.axis_index("mp") // 2
        blocks = partial.reshape(ny, 2, rows, partial.shape[1])
        mine = lax.dynamic_index_in_dim(blocks, core, 1, keepdims=False)
        other = lax.dynamic_index_in_dim(blocks, 1 - core, 1, keepdims=False)
        total = mine + core_swap(other)
        whole = lax.dynamic_index_in_dim(total, y_idx, 0, keepdims=False)
        for step in range(1, ny):
            away = lax.dynamic_index_in_dim(total, (y_idx + step) % ny, 0, keepdims=False)
            whole = whole + y_shift(away, step)
        return whole

    def gather_rows(piece):
        y_idx = lax.axis_index("mp") // 2
        if ny == 2:
            away = y_shift(piece, 1)
            column = jnp.where(
                y_idx == 0, jnp.stack([piece, away]), jnp.stack([away, piece])
            )
        else:
            column = jnp.zeros((ny,) + piece.shape, piece.dtype)
            column = lax.dynamic_update_index_in_dim(column, piece, y_idx, 0)
            for step in range(1, ny):
                away = y_shift(piece, step)
                column = lax.dynamic_update_index_in_dim(column, away, (y_idx - step) % ny, 0)
        both = by_core(column[:, None], core_swap(column)[:, None], 1)
        return both.reshape(mp * piece.shape[0], piece.shape[1])

    def gather_images(half):
        pieces = [half]
        for step in range(1, hi):
            pieces.append(lax.ppermute(half, "dp", [(i, (i - lo * step) % dp) for i in range(dp)]))
        column = jnp.stack(pieces)
        away = lax.ppermute(column, "dp", [(i, i ^ 1) for i in range(dp)])
        return column, away, core_swap(column), core_swap(away)

    def body(
        interface,
        latents,
        keep_mask,
        read_gain_lat,
        read_gain_int,
        read_query,
        read_keyval,
        read_out,
        read_gain_mlp,
        read_up,
        read_down,
        self_gain_att,
        self_qkv,
        self_out,
        self_gain_mlp,
        self_up,
        self_down,
        write_gain_int,
        write_gain_lat,
        write_query,
        write_keyval,
        write_out,
        write_gain_mlp,
        write_up,
        write_down,
        grad_interface_out,
        grad_latents_out,
    ):
        images = keep_mask.shape[0]
        layers = self_up.shape[0]
        shard_rows = interface.shape[0]
        lat_rows = latents.shape[0]
        latent_head = latents.shape[1] // HEADS
        patch_head = interface.shape[1] // HEADS
        own_rows = mp * lat_rows // images
        all_rows = dp * mp * lat_rows
        everywhere = images == 1 and dp % 2 == 0 and all_rows <= 2048
        mp_idx = lax.axis_index("mp")

        def spread(half):
            return gather_images(half) if everywhere else None

        def slow_mlp_weights(z, d, gain, w_up, w_down):
            n = layer_norm(z, gain)
            hidden, pull = gelu_pair(product(n, w_up))
            (du,) = pull(contract_last(d, w_down))
            return lax.psum((contract_rows(n, du), contract_rows(hidden, d)), "dp")

        def slow_att_weights(z, d, gain, w_qkv, w_out):
            n = layer_norm(z, gain)
            mix, back = jax.vjp(lambda *w: attend_self(n, *w), w_qkv[0], w_qkv[1], w_qkv[2])
            three = back(contract_last(d, w_out))
            return lax.psum((jnp.stack(three), contract_rows(mix, d)), "dp")

        def own_latents(block):
            return lax.dynamic_slice_in_dim(block, mp_idx * lat_rows, lat_rows, 0)

        flat_keep = keep_mask.reshape(-1).astype(jnp.float32)
        keep_rows = lax.dynamic_slice_in_dim(flat_keep, mp_idx * shard_rows, shard_rows, 0)[:, None]
        read_bias = jnp.where(keep_mask > 0, 0.0, MASK_FILL).astype(jnp.float32)

        def attend_read(qn, kn, wq, wk, wv):
            return attention(product(qn, wq), product(kn, wk), product(kn, wv), read_bias, images, latent_head)

        def attend_self(n, wq, wk, wv):
            return attention(product(n, wq), product(n, wk), product(n, wv), None, n.shape[0] // own_rows, latent_head)

        def attend_write(qn, m, wq, wk, wv):
            return attention(product(qn, wq), product(m, wk), product(m, wv), None, images, patch_head)

        x0 = interface * keep_rows
        z0 = gather_rows(latents)
        x0_full = gather_rows(x0)
        x0_read = layer_norm(x0_full, read_gain_int)
        z0_norm = layer_norm(z0, read_gain_lat)
        mix_read, back_read = jax.vjp(
            attend_read, z0_norm, x0_read, read_query, read_keyval[0], read_keyval[1]
        )
        dp_idx = lax.axis_index("dp")
        where = jnp.stack([dp_idx // lo, dp_idx % lo, core_idx()]).astype(jnp.int32)
        read_up3, read_down3 = read_up[None], read_down[None]
        sums = sum_halves(*halves(product(mix_read, read_out)))
        z1, z1_half, pre_read, *parts = mlp_forward(
            where, z0, *sums, read_gain_mlp, read_up3, read_down3, 0
        )
        z1_sets = spread(z1_half)
        sums = sum_halves(*parts)
        z = z1
        kept = []
        for layer in range(layers):
            z_in, in_half, qkv, *parts = att_forward(
                where, z, *sums, self_gain_att[layer], self_qkv[layer], self_out[layer]
            )
            in_sets = spread(in_half)
            sums = sum_halves(*parts)
            z_mid, mid_half, pre, *parts = mlp_forward(
                where, z_in, *sums, self_gain_mlp[layer], self_up, self_down, layer
            )
            mid_sets = spread(mid_half)
            sums = sum_halves(*parts)
            kept.append((z_in, in_sets, qkv, z_mid, mid_sets, pre))
            z = z_mid
        z_out = z + by_core(*sums, 0)

        x0_write = layer_norm(x0_full, write_gain_int)
        m_norm = layer_norm(z_out, write_gain_lat)
        mix_write, back_write = jax.vjp(
            attend_write, x0_write, m_norm, write_query, write_keyval[0], write_keyval[1]
        )
        x1 = x0 + sum_rows(product(mix_write, write_out))
        x1_norm = gather_rows(layer_norm(x1, write_gain_mlp))
        hidden_w, pull_w = gelu_pair(product(x1_norm, write_up))
        interface_out = x1 + sum_rows(product(hidden_w, write_down))

        gx_full = gather_rows(grad_interface_out)
        (du_w,) = pull_w(contract_last(gx_full, write_down))
        dn_w = sum_rows(contract_last(du_w, write_up))
        _, pull_norm = jax.vjp(layer_norm, x1, write_gain_mlp)
        dx_norm, gain_write_mlp = pull_norm(dn_w)
        gx1 = grad_interface_out + dx_norm
        gx1_full = gather_rows(gx1)
        pulled = back_write(contract_last(gx1_full, write_out))
        sums = sum_halves(*halves(pulled[1]))
        dq_rows = sum_rows(pulled[0])
        _, pull_norm = jax.vjp(layer_norm, x0, write_gain_int)
        dx_q, gain_write_int = pull_norm(dq_rows)
        grad_x = gx1 + dx_q
        grads_write = lax.psum(
            (
                pulled[2],
                jnp.stack([pulled[3], pulled[4]]),
                contract_rows(mix_write, gx1_full),
                contract_rows(x1_norm, du_w),
                contract_rows(hidden_w, gx_full),
            ),
            "dp",
        )

        d = gather_rows(grad_latents_out)
        prev, prev_gain = z_out, write_gain_lat
        gains_att = [None] * layers
        gains_mlp = [None] * layers
        before_mlp = before_att = ()
        slow_mlp = [None] * layers
        slow_att = [None] * layers
        for layer in reversed(range(layers)):
            z_in, in_sets, qkv, z_mid, mid_sets, pre = kept[layer]
            d, d_half, gain, *parts = mlp_backward(
                where, d, *sums, prev, prev_gain, pre, self_up, self_down, layer
            )
            if layer == layers - 1:
                gain_write_lat = gain[0]
            else:
                gains_att[layer + 1] = gain[0]
            sums = sum_halves(*parts)
            d_sets = spread(d_half)
            if everywhere:
                before_mlp = mlp_weights(
                    where, mid_sets, d_sets, self_gain_mlp[layer], self_up, self_down, layer, before_mlp
                )
            else:
                slow_mlp[layer] = slow_mlp_weights(
                    z_mid, d, self_gain_mlp[layer], self_up[layer], self_down[layer]
                )
            d, d_half, gain, *parts = att_backward(
                where, d, *sums, z_mid, self_gain_mlp[layer], qkv, self_qkv[layer], self_out[layer]
            )
            gains_mlp[layer] = gain[0]
            sums = sum_halves(*parts)
            d_sets = spread(d_half)
            if everywhere:
                before_att = att_weights(
                    where, in_sets, d_sets, self_gain_att[layer], self_qkv, self_out, layer, before_att
                )
            else:
                slow_att[layer] = slow_att_weights(
                    z_in, d, self_gain_att[layer], self_qkv[layer], self_out[layer]
                )
            prev, prev_gain = z_in, self_gain_att[layer]
        d, d_half, gain, *parts = mlp_backward(
            where, d, *sums, prev, prev_gain, pre_read, read_up3, read_down3, 0
        )
        gains_att[0] = gain[0]
        sums = sum_halves(*parts)
        if everywhere:
            d_sets = spread(d_half)
            grad_read_up, grad_read_down = (
                one[0]
                for one in mlp_weights(
                    where, z1_sets, d_sets, read_gain_mlp, read_up3, read_down3, 0, ()
                )
            )
            self_up_grad, self_down_grad = before_mlp
            self_qkv_grad, self_out_grad = before_att
        else:
            grad_read_up, grad_read_down = slow_mlp_weights(
                z1, d, read_gain_mlp, read_up, read_down
            )
            self_up_grad = jnp.stack([one[0] for one in slow_mlp])
            self_down_grad = jnp.stack([one[1] for one in slow_mlp])
            self_qkv_grad = jnp.stack([one[0] for one in slow_att])
            self_out_grad = jnp.stack([one[1] for one in slow_att])

        _, pull_norm = jax.vjp(layer_norm, z1, read_gain_mlp)
        dz_norm, gain_read_mlp = pull_norm(by_core(*sums, 0))
        d = d + dz_norm
        pulled = back_read(contract_last(d, read_out))
        dn_lat = sum_rows(pulled[0])
        _, pull_norm = jax.vjp(layer_norm, latents, read_gain_lat)
        dz_lat, gain_read_lat = pull_norm(dn_lat)
        grad_latents = own_latents(d) + dz_lat
        dn_int = sum_rows(pulled[1])
        _, pull_norm = jax.vjp(layer_norm, x0, read_gain_int)
        dx_k, gain_read_int = pull_norm(dn_int)
        grad_interface = (grad_x + dx_k) * keep_rows
        grads_write, d = lax.optimization_barrier((grads_write, d))
        grads_read = lax.psum(
            (pulled[2], jnp.stack([pulled[3], pulled[4]]), contract_rows(mix_read, d)), "dp"
        )

        once = (mp_idx == 0).astype(jnp.float32)
        gains = lax.psum(
            (
                gain_read_lat,
                gain_read_int,
                gain_read_mlp * once,
                jnp.stack(gains_att) * once,
                jnp.stack(gains_mlp) * once,
                gain_write_int,
                gain_write_lat * once,
                gain_write_mlp,
            ),
            ("dp", "mp"),
        )
        return (
            interface_out,
            own_latents(z_out),
            grad_interface,
            grad_latents,
            gains[0],
            gains[1],
            grads_read[0],
            grads_read[1],
            grads_read[2],
            gains[2],
            grad_read_up,
            grad_read_down,
            gains[3],
            self_qkv_grad,
            self_out_grad,
            gains[4],
            self_up_grad,
            self_down_grad,
            gains[5],
            gains[6],
            grads_write[0],
            grads_write[1],
            grads_write[2],
            gains[7],
            grads_write[3],
            grads_write[4],
        )

    return body


def solution(mesh):
    rows = P(("dp", "mp"), None)
    columns = P(None, "mp")
    heads_in = P("mp", None)
    in_specs = (
        rows,
        rows,
        P("dp", None),
        P(),
        P(),
        columns,
        P(None, None, "mp"),
        heads_in,
        P(),
        columns,
        heads_in,
        P(),
        P(None, None, None, "mp"),
        P(None, "mp", None),
        P(),
        P(None, None, "mp"),
        P(None, "mp", None),
        P(),
        P(),
        columns,
        P(None, None, "mp"),
        heads_in,
        P(),
        columns,
        heads_in,
        rows,
        rows,
    )
    out_specs = (rows, rows, rows, rows) + in_specs[3:25]
    body = make_body(mesh.shape["dp"], mesh.shape["mp"])
    return jax.shard_map(body, mesh=mesh, in_specs=in_specs, out_specs=out_specs, check_vma=False)
```
